512 devices in a mesh: leaf: 128 (over y, z, core), rhs: 4 (over x).
Axes of the slice: x: 4, y: 8, z: 8, core: 2. Of those that a mesh axis runs over, the one named last changes fastest.
Arguments:
- rhs_block: float32 [65536, 1024], P('leaf', 'rhs'), may hold values from -6 to 6
- leaf_order: int32 [128, 512], P('leaf'), may hold values from 0 to 511, as said below
- leaf_inverse: float32 [65536, 512], P('leaf'), may hold values from -0.04 to 3, as said below
- leaf_basis: float32 [65536, 128], P('leaf'), may hold values from -0.09678524 to 0.09678524
- transfer: bfloat16 [128, 6, 128, 128], P('leaf'), may hold values from -0.05 to 1.25, as said below
- precision: bfloat16 [128, 7, 128, 128], P('leaf'), may hold values from -0.09 to 8, as said below
Outputs:
- solution: float32 [65536, 1024], P('leaf', 'rhs')
The draws below stay inside these ranges and needn't reach their ends.
Inputs may be any that keep to these rules, and one draw needn't show every extreme that they name: `leaf_order`: each row is a permutation of 0 to 511. `leaf_inverse`: each leaf's block of 512 x 512 entries is symmetric positive definite. transfer[b, k] is the same for all leaves b of one aligned group of 2 ** (k + 1) leaves. Every block is symmetric positive definite; precision[b, k] is the same for all leaves b of one aligned group of 2 ** (k + 1) leaves.
All inputs are finite; a program needn't handle non-finite values.
Results may differ from the reference program's by a relative error of at most 0.0003.
Values sent between devices are 32-bit elements; how exact they have to be, the bound alone decides.
A program may use at most 64 MiB of HBM per device.

```python
import jax
import jax.numpy as jnp
from jax import lax

R = 128
LEAF_PTS = 512
COLS_DEV = 256
LEVELS = 7
NPTS = 65536
N_LEAF = 128
N_RHS = 4


def symmetric_blocks(key, count, size, lowest, highest, spread):
    key_noise, key_diag = jax.random.split(key)
    noise_part = jax.random.uniform(key_noise, (count, size, size), jnp.float32, -spread, spread)
    upper_part = jnp.triu(noise_part, 1)
    symmetric = upper_part + jnp.swapaxes(upper_part, 1, 2)
    uniforms = jax.random.uniform(key_diag, (count, size), jnp.float32)
    diagonal = lowest * (highest / lowest) ** uniforms
    return symmetric + diagonal[:, :, None] * jnp.eye(size, dtype=jnp.float32)


def group_owners(depth):
    return jnp.right_shift(jnp.arange(N_LEAF, dtype=jnp.int32), depth + 1) * 2 ** (depth + 1)


def leaf_orders(key):
    keys = jax.random.split(jax.random.fold_in(key, 21), N_LEAF)
    return jax.vmap(lambda single: jax.random.permutation(single, LEAF_PTS))(keys).astype(jnp.int32)


def leaf_bases(key):
    key_common, key_own = jax.random.split(jax.random.fold_in(key, 22))
    limit = (3.0 / LEAF_PTS) ** 0.5
    shared = jax.random.uniform(key_common, (N_LEAF, LEAF_PTS, 1), jnp.float32, -1.2 * limit, 1.2 * limit)
    own = jax.random.uniform(key_own, (N_LEAF, LEAF_PTS, R), jnp.float32, -limit, limit)
    return 0.8 * shared + 0.3 * own


def draw_leaf_order(key, part):
    return leaf_orders(key)


def draw_leaf_basis(key, part):
    return leaf_bases(key).reshape(NPTS, R)


def draw_rhs_block(key, part):
    orders = leaf_orders(key)
    bases = leaf_bases(key)
    key_mix, key_noise = jax.random.split(jax.random.fold_in(key, 23))
    columns = COLS_DEV * N_RHS
    mixing_cols = jax.random.normal(key_mix, (R, columns), jnp.float32)
    mixing_cols = mixing_cols - jnp.mean(mixing_cols, axis=0, keepdims=True)
    common = 2.0 * (LEAF_PTS / R) ** 0.5 * jnp.einsum('npr,rc->npc', bases, mixing_cols, precision=lax.Precision.HIGHEST)
    noise = 0.8 * jax.random.normal(key_noise, (N_LEAF, LEAF_PTS, columns), jnp.float32)
    tree_rows = jnp.clip(noise + common, -6.0, 6.0)
    leaf_rows = jnp.arange(N_LEAF, dtype=jnp.int32)[:, None]
    placed = jnp.zeros_like(tree_rows).at[leaf_rows, orders].set(tree_rows)
    return placed.reshape(NPTS, columns)


def draw_leaf_inverse(key, part):
    blocks = symmetric_blocks(jax.random.fold_in(key, 11), N_LEAF, LEAF_PTS, 1.3, 3.0, 0.04)
    return blocks.reshape(NPTS, LEAF_PTS)


def draw_precision(key, part):
    stacked = []
    for depth in range(LEVELS):
        blocks = symmetric_blocks(jax.random.fold_in(key, 100 + depth), N_LEAF, R, 2.0, 8.0, 0.08)
        stacked.append(jnp.take(blocks, group_owners(depth), axis=0))
    return jnp.stack(stacked, axis=1).astype(jnp.bfloat16)


def draw_transfer(key, part):
    stacked = []
    for depth in range(LEVELS - 1):
        key_noise, key_diag = jax.random.split(jax.random.fold_in(key, 300 + depth))
        noise_part = jax.random.uniform(key_noise, (N_LEAF, R, R), jnp.float32, -0.04, 0.04)
        diagonal = jax.random.uniform(key_diag, (N_LEAF, R), jnp.float32, 0.8, 1.2)
        blocks = noise_part + diagonal[:, :, None] * jnp.eye(R, dtype=jnp.float32)
        stacked.append(jnp.take(blocks, group_owners(depth), axis=0))
    return jnp.stack(stacked, axis=1).astype(jnp.bfloat16)


def setup_inputs(seed: int = 0) -> dict:
    arg_keys = jax.random.split(jax.random.key(seed), 7)
    return {
        "rhs_block": draw_rhs_block(jax.random.fold_in(arg_keys[6], 71), 0),
        "leaf_order": draw_leaf_order(jax.random.fold_in(arg_keys[6], 71), 0),
        "leaf_inverse": draw_leaf_inverse(jax.random.fold_in(arg_keys[6], 71), 0),
        "leaf_basis": draw_leaf_basis(jax.random.fold_in(arg_keys[6], 71), 0),
        "transfer": draw_transfer(jax.random.fold_in(arg_keys[6], 71), 0),
        "precision": draw_precision(jax.random.fold_in(arg_keys[6], 71), 0),
    }


def batched(left_op, right_op):
    return jnp.einsum('nij,njk->nik', left_op, right_op, precision=lax.Precision.HIGHEST)

def flipped(matrix):
    return jnp.swapaxes(matrix, 1, 2)

def cholesky_solve(matrix, right_side):
    factor = jnp.linalg.cholesky(matrix)
    middle = lax.linalg.triangular_solve(factor, right_side, left_side=True, lower=True)
    return lax.linalg.triangular_solve(factor, middle, left_side=True, lower=True, transpose_a=True)

def reference(rhs_block, leaf_order, leaf_inverse, leaf_basis, transfer, precision):
    leaves = N_LEAF
    points = LEAF_PTS
    columns = rhs_block.shape[1]
    ordered = rhs_block.reshape(leaves, points, columns)
    ordered = jnp.take_along_axis(ordered, leaf_order[:, :, None].astype(jnp.int32), axis=1)
    inverse = leaf_inverse.reshape(leaves, points, points)
    basis = leaf_basis.reshape(leaves, points, R)
    solved = batched(inverse, ordered)
    carried = batched(inverse, basis)
    projected = batched(flipped(basis), solved)
    gram_sum = batched(flipped(basis), carried)
    mixing = jnp.broadcast_to(jnp.eye(R, dtype=jnp.float32), (leaves, R, R))
    accumulated = jnp.zeros((leaves, R, columns), jnp.float32)
    for height in range(LEVELS):
        nodes_now = leaves >> height
        group_size = 2 ** (height + 1)
        summed = projected.reshape(nodes_now // 2, 2, R, columns).sum(axis=1)
        whole_gram = gram_sum.reshape(nodes_now // 2, 2, R, R).sum(axis=1)
        coupling = precision[::group_size, height].astype(jnp.float32)
        coeffs = cholesky_solve(coupling + whole_gram, jnp.concatenate([summed, coupling], axis=2))
        coef_rhs = coeffs[:, :, :columns]
        coef_basis = coeffs[:, :, columns:]
        accumulated = accumulated + batched(mixing, jnp.repeat(coef_rhs, group_size, axis=0))
        if height + 1 < LEVELS:
            mixer = transfer[::group_size, height].astype(jnp.float32)
            update = batched(coef_basis, mixer)
            mixing = batched(mixing, jnp.repeat(update, group_size, axis=0))
            projected = batched(flipped(mixer), batched(coupling, coef_rhs))
            left_part = batched(flipped(mixer), batched(flipped(coef_basis), whole_gram))
            gram_sum = batched(left_part, mixer)
    solved = solved - batched(carried, accumulated)
    rows = jnp.arange(leaves, dtype=jnp.int32)[:, None]
    placed = jnp.zeros_like(solved).at[rows, leaf_order.astype(jnp.int32)].set(solved)
    return placed.reshape(leaves * points, columns)
```

```python
import functools

import jax
import jax.numpy as jnp
from jax import lax
from jax.experimental import pallas as pl
from jax.experimental.pallas import tpu as pltpu
from jax.sharding import PartitionSpec as P

MESH = pl.DeviceIdType.MESH
F32 = jnp.float32
BF16 = jnp.bfloat16


def split(value):
    high = value.astype(BF16)
    return high, (value - high.astype(F32)).astype(BF16)


def dot(left, right, dims=((1,), (0,))):
    return lax.dot_general(left, right, (dims, ((), ())), preferred_element_type=F32)


def product(left, right, dims=((1,), (0,))):
    left_cat = jnp.concatenate([left[0], left[0], left[1]], axis=dims[0][0])
    right_cat = jnp.concatenate([right[0], right[1], right[0]], axis=dims[1][0])
    return dot(left_cat, right_cat, dims)


def inverse(blocks, ones):
    blocks = list(blocks)
    count = len(blocks)
    width = blocks[0].shape[1]
    sub = lax.broadcasted_iota(jnp.int32, (8, width), 0)
    lane = lax.broadcasted_iota(jnp.int32, (8, width), 1)
    for step in range(count):
        low = 8 * step
        rows = blocks[step]
        cols = [
            [jnp.broadcast_to(blocks[b][:, low + j : low + j + 1], (8, width)) for b in range(count)]
            for j in range(8)
        ]
        inside = (lane >= low) & (lane < low + 8)
        z = jnp.where(inside, jnp.where(lane - low == sub, 1.0, 0.0), rows)
        cb = [cols[k][step] * ones for k in range(8)]
        scale = ones
        for i in range(8):
            pivot = sub == i
            inv = 1.0 / jnp.broadcast_to(cb[i][i : i + 1, :], (8, width))
            m = jnp.where(pivot, 0.0, cb[i] * inv)
            scale = jnp.where(pivot, inv, scale)
            z = z - m * jnp.broadcast_to(z[i : i + 1, :], (8, width))
            for k in range(i + 1, 8):
                cb[k] = cb[k] - m * jnp.broadcast_to(cb[k][i : i + 1, :], (8, width))
        z = z * scale
        zr = [jnp.broadcast_to(z[j : j + 1, :], (8, width)) for j in range(8)]
        for turn in range(1, count):
            b = (step + turn) % count
            total = jnp.where(inside, 0.0, blocks[b])
            for j in range(8):
                total = total - cols[j][b] * zr[j]
            blocks[b] = total
        blocks[step] = z
    return blocks


def kernel(
    levels, rhs_ref, order_ref, inv_ref, basis_ref, transfer_ref, precision_ref, out_ref,
    gs, gr, ph, ps, pr, uh, ul, vh, vl, cc, minv, acc, mix, accr, zh, qin, onehot,
    ssem_g, rsem_g, ssem_p, rsem_p, sem_a,
):
    me = lax.axis_index("leaf")
    group = lax.axis_index("rhs")
    core = me % 2
    sibling = me + 1 - 2 * core

    def partner_of(apart, target):
        chip_partner = me + apart * (1 - 2 * ((me // apart) % 2))
        return (chip_partner // 2) * 2 + target

    def gram_copy(level, slot, target):
        return pltpu.make_async_remote_copy(
            src_ref=gs.at[level], dst_ref=gr.at[level], send_sem=ssem_g.at[level, slot], recv_sem=rsem_g.at[level],
            device_id=(target, group), device_id_type=MESH,
        )

    def proj_copy(level, target):
        return pltpu.make_async_remote_copy(
            src_ref=ps.at[level], dst_ref=pr.at[level], send_sem=ssem_p.at[level], recv_sem=rsem_p.at[level],
            device_id=(target, group), device_id_type=MESH,
        )

    barrier = pltpu.get_barrier_semaphore()
    pl.semaphore_signal(barrier, inc=1, device_id=(sibling, group), device_id_type=MESH)
    for level in range(1, levels):
        apart = 1 << level
        pl.semaphore_signal(barrier, inc=1, device_id=(partner_of(apart, 1), group), device_id_type=MESH)

        @pl.when(core == 0)
        def _():
            pl.semaphore_signal(barrier, inc=1, device_id=(partner_of(apart, 0), group), device_id_type=MESH)

    basis = split(basis_ref[...])
    leaf_inv = split(inv_ref[...])
    q = product(leaf_inv, basis)
    q_pair = split(q)
    gs[0] = product(basis, q_pair, ((0,), (0,)))

    @pl.when(core == 0)
    def _():
        pl.semaphore_wait(barrier, levels)

    @pl.when(core == 1)
    def _():
        pl.semaphore_wait(barrier, 2 * levels - 1)

    gram_copy(0, 0, sibling).start()

    points = rhs_ref.shape[0]
    order_row = order_ref[...]
    spread = lax.broadcasted_iota(jnp.int32, (points, points), 0) == order_row
    onehot[...] = jnp.where(spread, 1.0, 0.0).astype(BF16)
    q_in = (dot(onehot[...], q_pair[0]), dot(onehot[...], q_pair[1]))
    q_in = (q_in[0].astype(BF16), q_in[1].astype(BF16))
    qin[0] = q_in[0]
    qin[1] = q_in[1]
    rhs = split(rhs_ref[...])
    proj = product(q_in, rhs, ((0,), (0,)))
    ph[0] = proj[:, :128]
    ph[1] = proj[:, 128:]
    ps[0] = ph[1 - core]
    proj_copy(0, sibling).start()

    def tables(k, carry):
        mixer = transfer_ref[0, k]
        lam = precision_ref[0, k]
        u = dot(lam, mixer)
        v = dot(mixer, lam, ((0,), (0,)))
        u_pair = split(u)
        v_pair = split(v)
        uh[k] = u_pair[0]
        ul[k] = u_pair[1]
        vh[k] = v_pair[0]
        vl[k] = v_pair[1]
        cc[k] = dot(v_pair[0], mixer) + dot(v_pair[1], mixer)
        return carry

    lax.fori_loop(0, levels - 1, tables, 0)

    ordered = (
        dot(onehot[...], rhs[0], ((0,), (0,))).astype(BF16),
        dot(onehot[...], rhs[1], ((0,), (0,))).astype(BF16),
    )
    z = split(product(leaf_inv, ordered))
    z_in = dot(onehot[...], z[0]) + dot(onehot[...], z[1])
    zh[0] = z_in[:, :128]
    zh[1] = z_in[:, 128:]

    ones = jnp.where(zh[0, :8, :] == zh[0, :8, :], 1.0, 0.0)
    rank = acc.shape[0]
    acc[...] = jnp.zeros_like(acc)
    eye = lax.broadcasted_iota(jnp.int32, (rank, rank), 0) == lax.broadcasted_iota(jnp.int32, (rank, rank), 1)
    mix[...] = jnp.where(eye, 1.0, 0.0)

    def level_step(k, apart):
        gram_copy(k, 0, sibling).wait_recv()
        count = rank // 8
        blocks = []
        for b in range(count):
            at = pl.ds(8 * b, 8)
            blocks.append(precision_ref[0, k, at, :].astype(F32) + gs[k, at, :] + gr[k, at, :])
        for b, block in enumerate(inverse(blocks, ones)):
            minv[pl.ds(8 * b, 8), :] = block

        inv_pair = split(minv[...])
        following = 2 * apart

        @pl.when(k + 1 < levels)
        def _():
            y = split(product(inv_pair, (uh[k], ul[k])))
            gs[k + 1] = cc[k] - product((vh[k], vl[k]), y)

            @pl.when(core == 1)
            def _():
                gram_copy(k + 1, 0, partner_of(following, 1)).start()
                gram_copy(k + 1, 1, partner_of(following, 0)).start()

            uh[k] = y[0]
            ul[k] = y[1]

        proj_copy(k, sibling).wait_recv()
        own = jnp.where(k == 0, ph[core], ps[k])
        alpha = split(product(inv_pair, split(own + pr[k])))

        @pl.when(k + 1 < levels)
        def _():
            ps[k + 1] = product((vh[k], vl[k]), alpha)
            proj_copy(k + 1, partner_of(following, core)).start()

        mixing = split(mix[...])
        acc[...] += product(mixing, alpha)

        @pl.when(k + 1 < levels)
        def _():
            mix[...] = product(mixing, (uh[k], ul[k]))

        return following

    lax.fori_loop(0, levels, level_step, 1)

    swap = pltpu.make_async_remote_copy(
        src_ref=acc, dst_ref=accr, send_sem=sem_a.at[0], recv_sem=sem_a.at[1],
        device_id=(sibling, group), device_id_type=MESH,
    )
    swap.start()
    q_in = (qin[0], qin[1])
    half = pl.ds(pl.multiple_of(core * 128, 128), 128)
    out_ref[:, half] = zh[core] - product(q_in, split(acc[...]))
    swap.wait_recv()
    other = pl.ds(pl.multiple_of((1 - core) * 128, 128), 128)
    out_ref[:, other] = zh[1 - core] - product(q_in, split(accr[...]))

    swap.wait_send()
    gram_copy(0, 0, sibling).wait_send()
    proj_copy(0, sibling).wait_send()
    for level in range(1, levels):
        proj_copy(level, partner_of(1 << level, core)).wait_send()

        @pl.when(core == 1)
        def _():
            gram_copy(level, 0, partner_of(1 << level, 1)).wait_send()
            gram_copy(level, 1, partner_of(1 << level, 0)).wait_send()


def body(rhs_block, leaf_order, leaf_inverse, leaf_basis, transfer, precision):
    points, columns = rhs_block.shape
    rank = leaf_basis.shape[1]
    levels = precision.shape[1]
    half = columns // 2
    vmem = pl.BlockSpec(memory_space=pltpu.VMEM)
    dma = pltpu.SemaphoreType.DMA
    return pl.pallas_call(
        functools.partial(kernel, levels),
        out_shape=jax.ShapeDtypeStruct((points, columns), F32),
        in_specs=[vmem] * 6,
        out_specs=vmem,
        scratch_shapes=[
            pltpu.VMEM((levels, rank, rank), F32),
            pltpu.VMEM((levels, rank, rank), F32),
            pltpu.VMEM((2, rank, half), F32),
            pltpu.VMEM((levels, rank, half), F32),
            pltpu.VMEM((levels, rank, half), F32),
            pltpu.VMEM((levels, rank, rank), BF16),
            pltpu.VMEM((levels, rank, rank), BF16),
            pltpu.VMEM((levels, rank, rank), BF16),
            pltpu.VMEM((levels, rank, rank), BF16),
            pltpu.VMEM((levels, rank, rank), F32),
            pltpu.VMEM((rank, rank), F32),
            pltpu.VMEM((rank, half), F32),
            pltpu.VMEM((rank, rank), F32),
            pltpu.VMEM((rank, half), F32),
            pltpu.VMEM((2, points, half), F32),
            pltpu.VMEM((2, points, rank), BF16),
            pltpu.VMEM((points, points), BF16),
            dma((levels, 2)),
            dma((levels,)),
            dma((levels,)),
            dma((levels,)),
            dma((2,)),
        ],
        compiler_params=pltpu.CompilerParams(collective_id=0, has_side_effects=True, vmem_limit_bytes=48 * 2**20),
        name="tree_solve",
    )(rhs_block, leaf_order, leaf_inverse, leaf_basis, transfer, precision)


def solution(mesh):
    placed = (
        P("leaf", "rhs"),
        P("leaf", None),
        P("leaf", None),
        P("leaf", None),
        P("leaf", None, None, None),
        P("leaf", None, None, None),
    )
    return jax.shard_map(
        body, mesh=mesh, in_specs=placed, out_specs=P("leaf", "rhs"), check_vma=False
    )
```

```python
import functools

import jax
import jax.numpy as jnp
from jax import lax
from jax.experimental import pallas as pl
from jax.experimental.pallas import tpu as pltpu
from jax.sharding import PartitionSpec as P

MESH = pl.DeviceIdType.MESH
F32 = jnp.float32
BF16 = jnp.bfloat16
FLIP = ((0,), (0,))


def split(value):
    high = value.astype(BF16)
    return high, (value - high.astype(F32)).astype(BF16)


def dot(left, right, dims=((1,), (0,))):
    return lax.dot_general(left, right, (dims, ((), ())), preferred_element_type=F32)


def product(left, right, dims=((1,), (0,))):
    left_cat = jnp.concatenate([left[0], left[0], left[1]], axis=dims[0][0])
    right_cat = jnp.concatenate([right[0], right[1], right[0]], axis=dims[1][0])
    return dot(left_cat, right_cat, dims)


def row(value, at):
    return jnp.broadcast_to(value[at : at + 1, :], value.shape)


def total_of(terms):
    while len(terms) > 1:
        terms = [a + b for a, b in zip(terms[::2], terms[1::2])] + ([terms[-1]] if len(terms) % 2 else [])
    return terms[0]


def factors(blocks, ones):
    blocks = list(blocks)
    count = len(blocks)
    width = blocks[0].shape[1]
    sub = lax.broadcasted_iota(jnp.int32, (8, width), 0)
    lane = lax.broadcasted_iota(jnp.int32, (8, width), 1)
    even = sub % 2 == 0
    first, second = [None] * count, [None] * count
    for panel in range(0, count, 2):
        low = 8 * panel
        raw = [
            [jnp.broadcast_to(blocks[b][:, low + j : low + j + 1], (8, width)) for b in range(panel, count)]
            for j in range(16)
        ]
        inside = (lane >= low) & (lane < low + 16)
        unit = [jnp.where(inside, jnp.where(lane - low - 8 * w == sub, 1.0, 0.0), blocks[panel + w]) for w in range(2)]
        z = list(unit)
        cb = [[raw[j][w] * ones for w in range(2)] for j in range(16)]
        straight, cross = [ones, ones], [ones, ones]
        for i in range(0, 16, 2):
            v, s = i // 8, i % 8
            a, b, c = row(cb[i][v], s), row(cb[i + 1][v], s), row(cb[i + 1][v], s + 1)
            r = 1.0 / (a * c - b * b)
            ar, br, cr = a * r, b * r, c * r
            pair = (sub == s) | (sub == s + 1)
            straight[v] = jnp.where(sub == s, cr, jnp.where(sub == s + 1, ar, straight[v]))
            cross[v] = jnp.where(pair, br, cross[v])
            m = []
            for w in range(2):
                m1 = (cb[i][w] * c - cb[i + 1][w] * b) * r
                m2 = (cb[i + 1][w] * a - cb[i][w] * b) * r
                if w == v:
                    m1, m2 = jnp.where(pair, 0.0, m1), jnp.where(pair, 0.0, m2)
                m.append((m1, m2))
            for k in range(i + 2, 16):
                x, y = row(cb[k][v], s), row(cb[k][v], s + 1)
                cb[k] = [cb[k][w] - (m[w][0] * x + m[w][1] * y) for w in range(2)]
            x, y = row(z[v], s), row(z[v], s + 1)
            z = [z[w] - (m[w][0] * x + m[w][1] * y) for w in range(2)]
        done = []
        for w in range(2):
            swapped = jnp.where(even, pltpu.roll(z[w], 7, 0), pltpu.roll(z[w], 1, 0))
            done.append(straight[w] * z[w] - cross[w] * swapped)
        keep = lane < low + 16
        for w in range(2):
            first[panel + w] = jnp.where(keep, unit[w], 0.0)
            second[panel + w] = jnp.where(keep, done[w], 0.0)
        if panel + 2 < count:
            zr = [row(done[j // 8], j % 8) for j in range(16)]
            for b in range(panel + 2, count):
                terms = [raw[j][b - panel] * zr[j] for j in range(16)]
                blocks[b] = jnp.where(inside, 0.0, blocks[b]) - total_of(terms)
    return first, second


def kernel(
    levels, rhs_hbm, order_hbm, inv_hbm, basis_hbm, transfer_hbm, precision_hbm, out_ref,
    rhs_ref, order_ref, inv_ref, basis_ref, transfer_ref, precision_ref,
    gs, gr, ph, ps, pr, pso, po, uh, ul, vh, vl, cc, wv, yh, acc, mix, accr, zh, qin, onehot,
    sem_in, ssem_g, rsem_g, ssem_p, rsem_p, ssem_x, rsem_x,
):
    me = lax.axis_index("leaf")
    group = lax.axis_index("rhs")
    core = me % 2
    sibling = me + 1 - 2 * core
    last = levels - 1
    rank = acc.shape[0]

    def partner_of(apart, target):
        chip_partner = me + apart * (1 - 2 * ((me // apart) % 2))
        return (chip_partner // 2) * 2 + target

    def remote(src, dst, send_sem, recv_sem, target):
        return pltpu.make_async_remote_copy(
            src_ref=src, dst_ref=dst, send_sem=send_sem, recv_sem=recv_sem,
            device_id=(target, group), device_id_type=MESH,
        )

    def gram_copy(level, slot, target):
        return remote(gs.at[level], gr.at[level], ssem_g.at[level, slot], rsem_g.at[level], target)

    def proj_copy(level, target):
        return remote(ps.at[level], pr.at[level], ssem_p.at[level], rsem_p.at[level], target)

    def top_copy(n):
        src = acc if n == 2 else ps.at[last]
        target = sibling if n else partner_of(1 << last, 1 - core)
        return remote(src, (po, pso, accr)[n], ssem_x.at[n], rsem_x.at[n], target)

    loads = [
        pltpu.make_async_copy(src, dst, sem_in.at[n])
        for n, (src, dst) in enumerate((
            (basis_hbm, basis_ref), (inv_hbm, inv_ref), (order_hbm, order_ref), (rhs_hbm, rhs_ref),
            (precision_hbm, precision_ref), (transfer_hbm, transfer_ref),
        ))
    ]
    for load in loads:
        load.start()

    barrier = pltpu.get_barrier_semaphore()

    def tell(target):
        pl.semaphore_signal(barrier, inc=1, device_id=(target, group), device_id_type=MESH)

    tell(sibling)
    for level in range(1, levels):
        tell(partner_of(1 << level, 1))

        @pl.when(core == 0)
        def _():
            tell(partner_of(1 << level, 0))

    @pl.when(core == 1)
    def _():
        tell(partner_of(1 << last, 0))

    loads[0].wait()
    loads[1].wait()
    basis = split(basis_ref[...])
    q_pair = split(product(split(inv_ref[...]), basis))
    gs[0] = product(basis, q_pair, FLIP)

    @pl.when(core == 0)
    def _():
        pl.semaphore_wait(barrier, levels + 1)

    @pl.when(core == 1)
    def _():
        pl.semaphore_wait(barrier, 2 * levels - 1)

    gram_copy(0, 0, sibling).start()

    points = rhs_ref.shape[0]
    loads[2].wait()
    loads[3].wait()
    spread = lax.broadcasted_iota(jnp.int32, (points, points), 0) == order_ref[...]
    onehot[...] = jnp.where(spread, 1.0, 0.0).astype(BF16)
    q_in = (dot(onehot[...], q_pair[0]).astype(BF16), dot(onehot[...], q_pair[1]).astype(BF16))
    qin[0] = q_in[0]
    qin[1] = q_in[1]
    proj = product(q_in, split(rhs_ref[...]), FLIP)
    ph[0] = proj[:, :128]
    ph[1] = proj[:, 128:]
    ps[0] = ph[1 - core]
    proj_copy(0, sibling).start()

    def tables(k, carry):
        mixer = transfer_ref[0, k]
        lam = precision_ref[0, k]
        u = split(dot(lam, mixer))
        v = split(dot(mixer, lam, FLIP))
        uh[k], ul[k] = u
        vh[k], vl[k] = v
        cc[k] = dot(v[0], mixer) + dot(v[1], mixer)
        return carry

    loads[4].wait()
    loads[5].wait()
    lax.fori_loop(0, last, tables, 0)
    ones = jnp.where(basis_ref[:8, :] == basis_ref[:8, :], 1.0, 0.0)
    acc[...] = jnp.zeros_like(acc)
    eye = lax.broadcasted_iota(jnp.int32, (rank, rank), 0) == lax.broadcasted_iota(jnp.int32, (rank, rank), 1)
    mix[...] = jnp.where(eye, 1.0, 0.0)

    def level_step(k, apart):
        following = 2 * apart

        @pl.when(k == last)
        def _():
            q_in = (qin[0], qin[1])
            zh[core] -= product(q_in, split(acc[...]))
            top_copy(2).wait_recv()
            zh[1 - core] -= product(q_in, split(accr[...]))
            q_top = split(product(q_in, split(mix[...])))
            qin[0] = q_top[0]
            qin[1] = q_top[1]

        gram_copy(k, 0, sibling).wait_recv()
        matrix = precision_ref[0, k].astype(F32) + gs[k] + gr[k]
        blocks = [matrix[8 * b : 8 * b + 8, :] for b in range(rank // 8)]
        first, second = factors(blocks, ones)
        w_pair = split(jnp.concatenate(first, axis=0))
        v_pair = split(jnp.concatenate(second, axis=0))
        wv[0], wv[1] = w_pair
        wv[2], wv[3] = v_pair

        @pl.when(k < last)
        def _():
            u_pair = (uh[k], ul[k])
            w_u = split(product((wv[0], wv[1]), u_pair))
            v_u = split(product((wv[2], wv[3]), u_pair))
            gs[k + 1] = cc[k] - product(w_u, v_u, FLIP)

            @pl.when(core == 1)
            def _():
                gram_copy(k + 1, 0, partner_of(following, 1)).start()
                gram_copy(k + 1, 1, partner_of(following, 0)).start()

            yh[0], yh[1] = v_u
            proj_copy(k, sibling).wait_recv()
            own = jnp.where(k == 0, ph[core], ps[k])
            v_s = split(product((wv[2], wv[3]), split(own + pr[k])))
            both = tuple(jnp.concatenate([yh[n], v_s[n]], axis=1) for n in range(2))
            y_alpha = product((wv[0], wv[1]), both, FLIP)
            alpha = split(y_alpha[:, rank:])
            ps[k + 1] = product((vh[k], vl[k]), alpha)
            proj_copy(k + 1, partner_of(following, core)).start()
            turned = split(mix[...])
            acc[...] += product(turned, alpha)

            @pl.when(k + 1 == last)
            def _():
                for n in range(3):
                    top_copy(n).start()

            mix[...] = product(turned, split(y_alpha[:, :rank]))

            @pl.when(k == 2)
            def _():
                rhs = split(rhs_ref[...])
                ordered = tuple(dot(onehot[...], part, FLIP).astype(BF16) for part in rhs)
                z = split(product(split(inv_ref[...]), ordered))
                z_in = dot(onehot[...], z[0]) + dot(onehot[...], z[1])
                zh[0] = z_in[:, :128]
                zh[1] = z_in[:, 128:]

        return following

    lax.fori_loop(0, levels, level_step, 1)

    proj_copy(last, sibling).wait_recv()
    top_copy(0).wait_recv()
    top_copy(1).wait_recv()
    s = split(jnp.concatenate([ps[last] + pr[last], pso[...] + po[...]], axis=1))
    alpha = product((wv[0], wv[1]), split(product((wv[2], wv[3]), s)), FLIP)
    q_top = (qin[0], qin[1])
    for n, part in enumerate((core, 1 - core)):
        at = pl.ds(pl.multiple_of(part * 128, 128), 128)
        out_ref[:, at] = zh[part] - product(q_top, split(alpha[:, 128 * n : 128 * n + 128]))

    gram_copy(0, 0, sibling).wait_send()
    proj_copy(0, sibling).wait_send()
    for level in range(1, levels):
        proj_copy(level, partner_of(1 << level, core)).wait_send()

        @pl.when(core == 1)
        def _():
            gram_copy(level, 0, partner_of(1 << level, 1)).wait_send()
            gram_copy(level, 1, partner_of(1 << level, 0)).wait_send()

    for n in range(3):
        top_copy(n).wait_send()


def body(rhs_block, leaf_order, leaf_inverse, leaf_basis, transfer, precision):
    points, columns = rhs_block.shape
    rank = leaf_basis.shape[1]
    levels = precision.shape[1]
    half = columns // 2
    args = (rhs_block, leaf_order, leaf_inverse, leaf_basis, transfer, precision)
    dma = pltpu.SemaphoreType.DMA
    square = (rank, rank)
    return pl.pallas_call(
        functools.partial(kernel, levels),
        out_shape=jax.ShapeDtypeStruct((points, columns), F32),
        in_specs=[pl.BlockSpec(memory_space=pltpu.HBM)] * 6,
        out_specs=pl.BlockSpec(memory_space=pltpu.VMEM),
        scratch_shapes=[
            *(pltpu.VMEM(arg.shape, arg.dtype) for arg in args),
            pltpu.VMEM((levels, *square), F32),
            pltpu.VMEM((levels, *square), F32),
            pltpu.VMEM((2, rank, half), F32),
            pltpu.VMEM((levels, rank, half), F32),
            pltpu.VMEM((levels, rank, half), F32),
            pltpu.VMEM((rank, half), F32),
            pltpu.VMEM((rank, half), F32),
            pltpu.VMEM((levels, *square), BF16),
            pltpu.VMEM((levels, *square), BF16),
            pltpu.VMEM((levels, *square), BF16),
            pltpu.VMEM((levels, *square), BF16),
            pltpu.VMEM((levels, *square), F32),
            pltpu.VMEM((4, *square), BF16),
            pltpu.VMEM((2, *square), BF16),
            pltpu.VMEM((rank, half), F32),
            pltpu.VMEM(square, F32),
            pltpu.VMEM((rank, half), F32),
            pltpu.VMEM((2, points, half), F32),
            pltpu.VMEM((2, points, rank), BF16),
            pltpu.VMEM((points, points), BF16),
            dma((6,)),
            dma((levels, 2)),
            dma((levels,)),
            dma((levels,)),
            dma((levels,)),
            dma((3,)),
            dma((3,)),
        ],
        compiler_params=pltpu.CompilerParams(collective_id=0, has_side_effects=True, vmem_limit_bytes=60 * 2**20),
        name="tree_solve",
    )(*args)


def solution(mesh):
    placed = (
        P("leaf", "rhs"),
        P("leaf", None),
        P("leaf", None),
        P("leaf", None),
        P("leaf", None, None, None),
        P("leaf", None, None, None),
    )
    return jax.shard_map(
        body, mesh=mesh, in_specs=placed, out_specs=P("leaf", "rhs"), check_vma=False
    )
```

```python
import functools

import jax
import jax.numpy as jnp
from jax import lax
from jax.experimental import pallas as pl
from jax.experimental.pallas import tpu as pltpu
from jax.sharding import PartitionSpec as P

MESH = pl.DeviceIdType.MESH
F32 = jnp.float32
BF16 = jnp.bfloat16
FLIP = ((0,), (0,))


def split(value):
    high = value.astype(BF16)
    return high, (value - high.astype(F32)).astype(BF16)


def dot(left, right, dims=((1,), (0,))):
    return lax.dot_general(left, right, (dims, ((), ())), preferred_element_type=F32)


def product(left, right, dims=((1,), (0,))):
    left_cat = jnp.concatenate([left[0], left[0], left[1]], axis=dims[0][0])
    right_cat = jnp.concatenate([right[0], right[1], right[0]], axis=dims[1][0])
    return dot(left_cat, right_cat, dims)


def row(value, at):
    return jnp.broadcast_to(value[at : at + 1, :], value.shape)


def total_of(terms):
    while len(terms) > 1:
        terms = [a + b for a, b in zip(terms[::2], terms[1::2])] + ([terms[-1]] if len(terms) % 2 else [])
    return terms[0]


def factors(matrix, ones):
    count = matrix.shape[0] // 8
    width = matrix.shape[1]
    blocks = [matrix[8 * b : 8 * b + 8, :] for b in range(count)]
    sub = lax.broadcasted_iota(jnp.int32, (8, width), 0)
    lane = lax.broadcasted_iota(jnp.int32, (8, width), 1)
    even = sub % 2 == 0
    first, second = [None] * count, [None] * count
    for panel in range(0, count, 2):
        low = 8 * panel
        near = min(panel + 4, count)
        raw = [
            [jnp.broadcast_to(blocks[b][:, low + j : low + j + 1], (8, width)) for b in range(panel, near)]
            for j in range(16)
        ]
        inside = (lane >= low) & (lane < low + 16)
        unit = [jnp.where(inside, jnp.where(lane - low - 8 * w == sub, 1.0, 0.0), blocks[panel + w]) for w in range(2)]
        z = list(unit)
        cb = [[raw[j][w] * ones for w in range(2)] for j in range(16)]
        straight, cross = [ones, ones], [ones, ones]
        for i in range(0, 16, 2):
            v, s = i // 8, i % 8
            a, b, c = row(cb[i][v], s), row(cb[i + 1][v], s), row(cb[i + 1][v], s + 1)
            r = 1.0 / (a * c - b * b)
            ar, br, cr = a * r, b * r, c * r
            pair = (sub == s) | (sub == s + 1)
            straight[v] = jnp.where(sub == s, cr, jnp.where(sub == s + 1, ar, straight[v]))
            cross[v] = jnp.where(pair, br, cross[v])
            m = []
            for w in range(2):
                m1 = (cb[i][w] * c - cb[i + 1][w] * b) * r
                m2 = (cb[i + 1][w] * a - cb[i][w] * b) * r
                if w == v:
                    m1, m2 = jnp.where(pair, 0.0, m1), jnp.where(pair, 0.0, m2)
                m.append((m1, m2))
            for k in range(i + 2, 16):
                x, y = row(cb[k][v], s), row(cb[k][v], s + 1)
                cb[k] = [cb[k][w] - (m[w][0] * x + m[w][1] * y) for w in range(2)]
            x, y = row(z[v], s), row(z[v], s + 1)
            z = [z[w] - (m[w][0] * x + m[w][1] * y) for w in range(2)]
        done = []
        for w in range(2):
            swapped = jnp.where(even, pltpu.roll(z[w], 7, 0), pltpu.roll(z[w], 1, 0))
            done.append(straight[w] * z[w] - cross[w] * swapped)
        keep = lane < low + 16
        for w in range(2):
            first[panel + w] = jnp.where(keep, unit[w], 0.0)
            second[panel + w] = jnp.where(keep, done[w], 0.0)
        zr = [row(done[j // 8], j % 8) for j in range(16)]
        for b in range(panel + 2, near):
            terms = [raw[j][b - panel] * zr[j] for j in range(16)]
            blocks[b] = jnp.where(inside, 0.0, blocks[b]) - total_of(terms)
        if near < count:
            far = jnp.concatenate(blocks[near:], axis=0)
            zero = jnp.zeros((8, width), F32)
            weights = jnp.concatenate([done[b - panel] if 0 <= b - panel < 2 else zero for b in range(count)], axis=0)
            change = jnp.dot(far, weights, precision=lax.Precision.HIGHEST, preferred_element_type=F32)
            for n, b in enumerate(range(near, count)):
                blocks[b] = jnp.where(inside, 0.0, blocks[b]) - change[8 * n : 8 * n + 8, :]
    return first, second


def kernel(
    levels, rhs_hbm, order_hbm, inv_hbm, basis_hbm, transfer_hbm, precision_hbm, out_ref,
    rhs_ref, order_ref, inv_ref, basis_ref, transfer_ref, precision_ref,
    gs, gr, ph, ps, pr, pso, po, uh, ul, vh, vl, cc, wv, yh, acc, mix, accr, zh, qin, onehot,
    sem_in, ssem_g, rsem_g, ssem_p, rsem_p, ssem_x, rsem_x,
):
    me = lax.axis_index("leaf")
    group = lax.axis_index("rhs")
    core = me % 2
    sibling = me + 1 - 2 * core
    last = levels - 1
    rank = acc.shape[0]

    def partner_of(apart, target):
        chip_partner = me + apart * (1 - 2 * ((me // apart) % 2))
        return (chip_partner // 2) * 2 + target

    def remote(src, dst, send_sem, recv_sem, target):
        return pltpu.make_async_remote_copy(
            src_ref=src, dst_ref=dst, send_sem=send_sem, recv_sem=recv_sem,
            device_id=(target, group), device_id_type=MESH,
        )

    def gram_copy(level, slot, target):
        return remote(gs.at[level], gr.at[level], ssem_g.at[level, slot], rsem_g.at[level], target)

    def proj_copy(level, target):
        return remote(ps.at[level], pr.at[level], ssem_p.at[level], rsem_p.at[level], target)

    def top_copy(n):
        src = acc if n == 2 else ps.at[last]
        target = sibling if n else partner_of(1 << last, 1 - core)
        return remote(src, (po, pso, accr)[n], ssem_x.at[n], rsem_x.at[n], target)

    loads = [
        pltpu.make_async_copy(src, dst, sem_in.at[n])
        for n, (src, dst) in enumerate((
            (basis_hbm, basis_ref), (inv_hbm, inv_ref), (order_hbm, order_ref), (rhs_hbm, rhs_ref),
            (precision_hbm, precision_ref), (transfer_hbm, transfer_ref),
        ))
    ]
    for load in loads:
        load.start()

    barrier = pltpu.get_barrier_semaphore()

    def tell(target):
        pl.semaphore_signal(barrier, inc=1, device_id=(target, group), device_id_type=MESH)

    tell(sibling)
    for level in range(1, levels):
        tell(partner_of(1 << level, 1))

        @pl.when(core == 0)
        def _():
            tell(partner_of(1 << level, 0))

    @pl.when(core == 1)
    def _():
        tell(partner_of(1 << last, 0))

    loads[0].wait()
    loads[1].wait()
    basis = split(basis_ref[...])
    q_pair = split(product(split(inv_ref[...]), basis))
    gs[0] = product(basis, q_pair, FLIP)

    @pl.when(core == 0)
    def _():
        pl.semaphore_wait(barrier, levels + 1)

    @pl.when(core == 1)
    def _():
        pl.semaphore_wait(barrier, 2 * levels - 1)

    gram_copy(0, 0, sibling).start()

    points = rhs_ref.shape[0]
    loads[2].wait()
    loads[3].wait()
    spread = lax.broadcasted_iota(jnp.int32, (points, points), 0) == order_ref[...]
    onehot[...] = jnp.where(spread, 1.0, 0.0).astype(BF16)
    q_in = (dot(onehot[...], q_pair[0]).astype(BF16), dot(onehot[...], q_pair[1]).astype(BF16))
    qin[0] = q_in[0]
    qin[1] = q_in[1]
    proj = product(q_in, split(rhs_ref[...]), FLIP)
    ph[0] = proj[:, :128]
    ph[1] = proj[:, 128:]
    ps[0] = ph[1 - core]
    proj_copy(0, sibling).start()

    def tables(k, carry):
        mixer = transfer_ref[0, k]
        lam = precision_ref[0, k]
        u = split(dot(lam, mixer))
        v = split(dot(mixer, lam, FLIP))
        uh[k], ul[k] = u
        vh[k], vl[k] = v
        cc[k] = dot(v[0], mixer) + dot(v[1], mixer)
        return carry

    loads[4].wait()
    loads[5].wait()
    tables(0, 0)
    ones = jnp.where(basis_ref[:8, :] == basis_ref[:8, :], 1.0, 0.0)
    acc[...] = jnp.zeros_like(acc)
    eye = lax.broadcasted_iota(jnp.int32, (rank, rank), 0) == lax.broadcasted_iota(jnp.int32, (rank, rank), 1)
    mix[...] = jnp.where(eye, 1.0, 0.0)

    def level_step(k, apart):
        following = 2 * apart

        @pl.when(k == last)
        def _():
            q_in = (qin[0], qin[1])
            zh[core] -= product(q_in, split(acc[...]))
            top_copy(2).wait_recv()
            zh[1 - core] -= product(q_in, split(accr[...]))
            q_top = split(product(q_in, split(mix[...])))
            qin[0] = q_top[0]
            qin[1] = q_top[1]

        gram_copy(k, 0, sibling).wait_recv()
        matrix = precision_ref[0, k].astype(F32) + gs[k] + gr[k]
        first, second = factors(matrix, ones)
        w_pair = split(jnp.concatenate(first, axis=0))
        v_pair = split(jnp.concatenate(second, axis=0))
        wv[0], wv[1] = w_pair
        wv[2], wv[3] = v_pair

        @pl.when(k < last)
        def _():
            u_pair = (uh[k], ul[k])
            w_u = split(product((wv[0], wv[1]), u_pair))
            v_u = split(product((wv[2], wv[3]), u_pair))
            gs[k + 1] = cc[k] - product(w_u, v_u, FLIP)

            @pl.when(core == 1)
            def _():
                gram_copy(k + 1, 0, partner_of(following, 1)).start()
                gram_copy(k + 1, 1, partner_of(following, 0)).start()

            yh[0], yh[1] = v_u
            proj_copy(k, sibling).wait_recv()
            own = jnp.where(k == 0, ph[core], ps[k])
            v_s = split(product((wv[2], wv[3]), split(own + pr[k])))
            both = tuple(jnp.concatenate([yh[n], v_s[n]], axis=1) for n in range(2))
            y_alpha = product((wv[0], wv[1]), both, FLIP)
            alpha = split(y_alpha[:, rank:])
            ps[k + 1] = product((vh[k], vl[k]), alpha)
            proj_copy(k + 1, partner_of(following, core)).start()
            turned = split(mix[...])
            acc[...] += product(turned, alpha)

            @pl.when(k + 1 == last)
            def _():
                for n in range(3):
                    top_copy(n).start()

            mix[...] = product(turned, split(y_alpha[:, :rank]))

            @pl.when(k == 0)
            def _():
                lax.fori_loop(1, 3, tables, 0)

            @pl.when(k == 1)
            def _():
                lax.fori_loop(3, last, tables, 0)

            @pl.when(k == 2)
            def _():
                rhs = split(rhs_ref[...])
                ordered = tuple(dot(onehot[...], part, FLIP).astype(BF16) for part in rhs)
                z = split(product(split(inv_ref[...]), ordered))
                z_in = dot(onehot[...], z[0]) + dot(onehot[...], z[1])
                zh[0] = z_in[:, :128]
                zh[1] = z_in[:, 128:]

        return following

    lax.fori_loop(0, levels, level_step, 1)

    proj_copy(last, sibling).wait_recv()
    top_copy(0).wait_recv()
    top_copy(1).wait_recv()
    s = split(jnp.concatenate([ps[last] + pr[last], pso[...] + po[...]], axis=1))
    alpha = product((wv[0], wv[1]), split(product((wv[2], wv[3]), s)), FLIP)
    q_top = (qin[0], qin[1])
    for n, part in enumerate((core, 1 - core)):
        at = pl.ds(pl.multiple_of(part * 128, 128), 128)
        out_ref[:, at] = zh[part] - product(q_top, split(alpha[:, 128 * n : 128 * n + 128]))

    gram_copy(0, 0, sibling).wait_send()
    proj_copy(0, sibling).wait_send()
    for level in range(1, levels):
        proj_copy(level, partner_of(1 << level, core)).wait_send()

        @pl.when(core == 1)
        def _():
            gram_copy(level, 0, partner_of(1 << level, 1)).wait_send()
            gram_copy(level, 1, partner_of(1 << level, 0)).wait_send()

    for n in range(3):
        top_copy(n).wait_send()


def body(rhs_block, leaf_order, leaf_inverse, leaf_basis, transfer, precision):
    points, columns = rhs_block.shape
    rank = leaf_basis.shape[1]
    levels = precision.shape[1]
    half = columns // 2
    args = (rhs_block, leaf_order, leaf_inverse, leaf_basis, transfer, precision)
    dma = pltpu.SemaphoreType.DMA
    square = (rank, rank)
    return pl.pallas_call(
        functools.partial(kernel, levels),
        out_shape=jax.ShapeDtypeStruct((points, columns), F32),
        in_specs=[pl.BlockSpec(memory_space=pltpu.HBM)] * 6,
        out_specs=pl.BlockSpec(memory_space=pltpu.VMEM),
        scratch_shapes=[
            *(pltpu.VMEM(arg.shape, arg.dtype) for arg in args),
            pltpu.VMEM((levels, *square), F32),
            pltpu.VMEM((levels, *square), F32),
            pltpu.VMEM((2, rank, half), F32),
            pltpu.VMEM((levels, rank, half), F32),
            pltpu.VMEM((levels, rank, half), F32),
            pltpu.VMEM((rank, half), F32),
            pltpu.VMEM((rank, half), F32),
            pltpu.VMEM((levels, *square), BF16),
            pltpu.VMEM((levels, *square), BF16),
            pltpu.VMEM((levels, *square), BF16),
            pltpu.VMEM((levels, *square), BF16),
            pltpu.VMEM((levels, *square), F32),
            pltpu.VMEM((4, *square), BF16),
            pltpu.VMEM((2, *square), BF16),
            pltpu.VMEM((rank, half), F32),
            pltpu.VMEM(square, F32),
            pltpu.VMEM((rank, half), F32),
            pltpu.VMEM((2, points, half), F32),
            pltpu.VMEM((2, points, rank), BF16),
            pltpu.VMEM((points, points), BF16),
            dma((6,)),
            dma((levels, 2)),
            dma((levels,)),
            dma((levels,)),
            dma((levels,)),
            dma((3,)),
            dma((3,)),
        ],
        compiler_params=pltpu.CompilerParams(collective_id=0, has_side_effects=True, vmem_limit_bytes=60 * 2**20),
        name="tree_solve",
    )(*args)


def solution(mesh):
    placed = (
        P("leaf", "rhs"),
        P("leaf", None),
        P("leaf", None),
        P("leaf", None),
        P("leaf", None, None, None),
        P("leaf", None, None, None),
    )
    return jax.shard_map(
        body, mesh=mesh, in_specs=placed, out_specs=P("leaf", "rhs"), check_vma=False
    )
```

```python
import functools

import jax
import jax.numpy as jnp
from jax import lax
from jax.experimental import pallas as pl
from jax.experimental.pallas import tpu as pltpu
from jax.sharding import PartitionSpec as P

MESH = pl.DeviceIdType.MESH
F32 = jnp.float32
BF16 = jnp.bfloat16
FLIP = ((0,), (0,))


def split(value):
    high = value.astype(BF16)
    return high, (value - high.astype(F32)).astype(BF16)


def dot(left, right, dims=((1,), (0,))):
    return lax.dot_general(left, right, (dims, ((), ())), preferred_element_type=F32)


def product(left, right, dims=((1,), (0,))):
    left_cat = jnp.concatenate([left[0], left[0], left[1]], axis=dims[0][0])
    right_cat = jnp.concatenate([right[0], right[1], right[0]], axis=dims[1][0])
    return dot(left_cat, right_cat, dims)


def row(value, at):
    return jnp.broadcast_to(value[at : at + 1, :], value.shape)


def total_of(terms):
    while len(terms) > 1:
        terms = [a + b for a, b in zip(terms[::2], terms[1::2])] + ([terms[-1]] if len(terms) % 2 else [])
    return terms[0]


def factors(matrix, ones):
    count = matrix.shape[0] // 8
    width = matrix.shape[1]
    blocks = [matrix[8 * b : 8 * b + 8, :] for b in range(count)]
    sub = lax.broadcasted_iota(jnp.int32, (8, width), 0)
    lane = lax.broadcasted_iota(jnp.int32, (8, width), 1)
    even = sub % 2 == 0
    first, second = [None] * count, [None] * count
    for panel in range(0, count, 2):
        low = 8 * panel
        near = min(panel + 4, count)
        raw = [
            [jnp.broadcast_to(blocks[b][:, low + j : low + j + 1], (8, width)) for b in range(panel, near)]
            for j in range(16)
        ]
        inside = (lane >= low) & (lane < low + 16)
        unit = [jnp.where(inside, jnp.where(lane - low - 8 * w == sub, 1.0, 0.0), blocks[panel + w]) for w in range(2)]
        z = list(unit)
        cb = [[raw[j][w] * ones for w in range(2)] for j in range(16)]
        straight, cross = [ones, ones], [ones, ones]
        for i in range(0, 16, 2):
            v, s = i // 8, i % 8
            a, b, c = row(cb[i][v], s), row(cb[i + 1][v], s), row(cb[i + 1][v], s + 1)
            r = 1.0 / (a * c - b * b)
            ar, br, cr = a * r, b * r, c * r
            pair = (sub == s) | (sub == s + 1)
            straight[v] = jnp.where(sub == s, cr, jnp.where(sub == s + 1, ar, straight[v]))
            cross[v] = jnp.where(pair, br, cross[v])
            m = []
            for w in range(2):
                m1 = (cb[i][w] * c - cb[i + 1][w] * b) * r
                m2 = (cb[i + 1][w] * a - cb[i][w] * b) * r
                if w == v:
                    m1, m2 = jnp.where(pair, 0.0, m1), jnp.where(pair, 0.0, m2)
                m.append((m1, m2))
            for k in range(i + 2, 16):
                x, y = row(cb[k][v], s), row(cb[k][v], s + 1)
                cb[k] = [cb[k][w] - (m[w][0] * x + m[w][1] * y) for w in range(2)]
            x, y = row(z[v], s), row(z[v], s + 1)
            z = [z[w] - (m[w][0] * x + m[w][1] * y) for w in range(2)]
        done = []
        for w in range(2):
            swapped = jnp.where(even, pltpu.roll(z[w], 7, 0), pltpu.roll(z[w], 1, 0))
            done.append(straight[w] * z[w] - cross[w] * swapped)
        keep = lane < low + 16
        for w in range(2):
            first[panel + w] = jnp.where(keep, unit[w], 0.0)
            second[panel + w] = jnp.where(keep, done[w], 0.0)
        zr = [row(done[j // 8], j % 8) for j in range(16)]
        for b in range(panel + 2, near):
            terms = [raw[j][b - panel] * zr[j] for j in range(16)]
            blocks[b] = jnp.where(inside, 0.0, blocks[b]) - total_of(terms)
        if near < count:
            far = jnp.concatenate(blocks[near:], axis=0)
            zero = jnp.zeros((8, width), F32)
            weights = jnp.concatenate([done[b - panel] if 0 <= b - panel < 2 else zero for b in range(count)], axis=0)
            change = jnp.dot(far, weights, precision=lax.Precision.HIGHEST, preferred_element_type=F32)
            for n, b in enumerate(range(near, count)):
                blocks[b] = jnp.where(inside, 0.0, blocks[b]) - change[8 * n : 8 * n + 8, :]
    return first, second


def kernel(
    levels, rhs_hbm, order_hbm, inv_hbm, basis_hbm, transfer_hbm, precision_hbm, z_out, q_out, alpha_ref,
    rhs_ref, order_ref, inv_ref, basis_ref, transfer_ref, precision_ref,
    gs, gr, ph, ps, pr, pso, po, uh, ul, vh, vl, cc, wv, yh, acc, mix, accr, zh, qin, qf, onehot,
    sem_in, sem_out, ssem_g, rsem_g, ssem_p, rsem_p, ssem_x, rsem_x,
):
    me = lax.axis_index("leaf")
    group = lax.axis_index("rhs")
    core = me % 2
    sibling = me + 1 - 2 * core
    last = levels - 1
    rank = acc.shape[0]

    def partner_of(apart, target):
        chip_partner = me + apart * (1 - 2 * ((me // apart) % 2))
        return (chip_partner // 2) * 2 + target

    def remote(src, dst, send_sem, recv_sem, target):
        return pltpu.make_async_remote_copy(
            src_ref=src, dst_ref=dst, send_sem=send_sem, recv_sem=recv_sem,
            device_id=(target, group), device_id_type=MESH,
        )

    def gram_copy(level, slot, target):
        return remote(gs.at[level], gr.at[level], ssem_g.at[level, slot], rsem_g.at[level], target)

    def pass_on(level):
        return remote(gr.at[level], gr.at[level], ssem_g.at[level, 1], rsem_g.at[level], sibling)

    def proj_copy(level, target):
        return remote(ps.at[level], pr.at[level], ssem_p.at[level], rsem_p.at[level], target)

    def top_copy(n):
        src = acc if n == 2 else ps.at[last]
        target = sibling if n else partner_of(1 << last, 1 - core)
        return remote(src, (po, pso, accr)[n], ssem_x.at[n], rsem_x.at[n], target)

    def result_copy(n):
        src = qf if n == 2 else zh.at[n]
        dst = q_out if n == 2 else z_out.at[:, pl.ds(128 * n, 128)]
        return pltpu.make_async_copy(src, dst, sem_out.at[n])

    loads = [
        pltpu.make_async_copy(src, dst, sem_in.at[n])
        for n, (src, dst) in enumerate((
            (basis_hbm, basis_ref), (inv_hbm, inv_ref), (order_hbm, order_ref), (rhs_hbm, rhs_ref),
            (precision_hbm, precision_ref), (transfer_hbm, transfer_ref),
        ))
    ]
    for load in loads:
        load.start()

    barrier = pltpu.get_barrier_semaphore()

    def tell(target):
        pl.semaphore_signal(barrier, inc=1, device_id=(target, group), device_id_type=MESH)

    tell(sibling)
    for level in range(1, levels):
        tell(partner_of(1 << level, core))
    tell(partner_of(1 << last, 1 - core))

    loads[0].wait()
    loads[1].wait()
    basis = split(basis_ref[...])
    q_pair = split(product(split(inv_ref[...]), basis))
    gs[0] = product(basis, q_pair, FLIP)

    pl.semaphore_wait(barrier, levels + 1)
    gram_copy(0, 0, sibling).start()

    points = rhs_ref.shape[0]
    loads[2].wait()
    loads[3].wait()
    spread = lax.broadcasted_iota(jnp.int32, (points, points), 0) == order_ref[...]
    onehot[...] = jnp.where(spread, 1.0, 0.0).astype(BF16)
    q_in = (dot(onehot[...], q_pair[0]).astype(BF16), dot(onehot[...], q_pair[1]).astype(BF16))
    qin[0] = q_in[0]
    qin[1] = q_in[1]
    proj = product(q_in, split(rhs_ref[...]), FLIP)
    ph[0] = proj[:, :128]
    ph[1] = proj[:, 128:]
    ps[0] = ph[1 - core]
    proj_copy(0, sibling).start()

    def tables(k, carry):
        mixer = transfer_ref[0, k]
        lam = precision_ref[0, k]
        u = split(dot(lam, mixer))
        v = split(dot(mixer, lam, FLIP))
        uh[k], ul[k] = u
        vh[k], vl[k] = v
        cc[k] = dot(v[0], mixer) + dot(v[1], mixer)
        return carry

    loads[4].wait()
    loads[5].wait()
    tables(0, 0)
    ones = jnp.where(basis_ref[:8, :] == basis_ref[:8, :], 1.0, 0.0)
    acc[...] = jnp.zeros_like(acc)
    eye = lax.broadcasted_iota(jnp.int32, (rank, rank), 0) == lax.broadcasted_iota(jnp.int32, (rank, rank), 1)
    mix[...] = jnp.where(eye, 1.0, 0.0)

    def level_step(k, apart):
        following = 2 * apart

        @pl.when(k == last)
        def _():
            q_in = (qin[0], qin[1])
            zh[core] -= product(q_in, split(acc[...]))
            top_copy(2).wait_recv()
            zh[1 - core] -= product(q_in, split(accr[...]))
            qf[...] = product(q_in, split(mix[...]))
            for n in range(3):
                result_copy(n).start()

        gram_copy(k, 0, sibling).wait_recv()

        @pl.when((core == 1) & (k > 0) & (k < last))
        def _():
            pass_on(k).start()

        matrix = precision_ref[0, k].astype(F32) + gs[k] + gr[k]
        first, second = factors(matrix, ones)
        w_pair = split(jnp.concatenate(first, axis=0))
        v_pair = split(jnp.concatenate(second, axis=0))
        wv[0], wv[1] = w_pair
        wv[2], wv[3] = v_pair

        @pl.when(k < last)
        def _():
            u_pair = (uh[k], ul[k])
            w_u = split(product((wv[0], wv[1]), u_pair))
            v_u = split(product((wv[2], wv[3]), u_pair))
            gs[k + 1] = cc[k] - product(w_u, v_u, FLIP)

            @pl.when(core == 1)
            def _():
                gram_copy(k + 1, 0, partner_of(following, 1)).start()

                @pl.when(k + 1 == last)
                def _():
                    gram_copy(last, 1, partner_of(following, 0)).start()

            yh[0], yh[1] = v_u
            proj_copy(k, sibling).wait_recv()
            own = jnp.where(k == 0, ph[core], ps[k])
            v_s = split(product((wv[2], wv[3]), split(own + pr[k])))
            both = tuple(jnp.concatenate([yh[n], v_s[n]], axis=1) for n in range(2))
            y_alpha = product((wv[0], wv[1]), both, FLIP)
            alpha = split(y_alpha[:, rank:])
            ps[k + 1] = product((vh[k], vl[k]), alpha)
            proj_copy(k + 1, partner_of(following, core)).start()
            turned = split(mix[...])
            acc[...] += product(turned, alpha)

            @pl.when(k + 1 == last)
            def _():
                for n in range(3):
                    top_copy(n).start()

            mix[...] = product(turned, split(y_alpha[:, :rank]))

            @pl.when(k == 0)
            def _():
                lax.fori_loop(1, 3, tables, 0)

            @pl.when(k == 1)
            def _():
                lax.fori_loop(3, last, tables, 0)

            @pl.when(k == 2)
            def _():
                rhs = split(rhs_ref[...])
                ordered = tuple(dot(onehot[...], part, FLIP).astype(BF16) for part in rhs)
                z = split(product(split(inv_ref[...]), ordered))
                z_in = dot(onehot[...], z[0]) + dot(onehot[...], z[1])
                zh[0] = z_in[:, :128]
                zh[1] = z_in[:, 128:]

        return following

    lax.fori_loop(0, levels, level_step, 1)

    proj_copy(last, sibling).wait_recv()
    top_copy(0).wait_recv()
    top_copy(1).wait_recv()
    s = split(jnp.concatenate([ps[last] + pr[last], pso[...] + po[...]], axis=1))
    alpha = product((wv[0], wv[1]), split(product((wv[2], wv[3]), s)), FLIP)
    for n, part in enumerate((core, 1 - core)):
        at = pl.ds(pl.multiple_of(part * 128, 128), 128)
        alpha_ref[:, at] = alpha[:, 128 * n : 128 * n + 128]

    for n in range(3):
        result_copy(n).wait()
    gram_copy(0, 0, sibling).wait_send()
    proj_copy(0, sibling).wait_send()
    for level in range(1, levels):
        proj_copy(level, partner_of(1 << level, core)).wait_send()

        @pl.when(core == 1)
        def _():
            gram_copy(level, 0, partner_of(1 << level, 1)).wait_send()
            if level == last:
                gram_copy(level, 1, partner_of(1 << level, 0)).wait_send()
            else:
                pass_on(level).wait_send()

    for n in range(3):
        top_copy(n).wait_send()


def body(rhs_block, leaf_order, leaf_inverse, leaf_basis, transfer, precision):
    points, columns = rhs_block.shape
    rank = leaf_basis.shape[1]
    levels = precision.shape[1]
    half = columns // 2
    args = (rhs_block, leaf_order, leaf_inverse, leaf_basis, transfer, precision)
    dma = pltpu.SemaphoreType.DMA
    square = (rank, rank)
    z, q, alpha = pl.pallas_call(
        functools.partial(kernel, levels),
        out_shape=[
            jax.ShapeDtypeStruct((points, columns), F32),
            jax.ShapeDtypeStruct((points, rank), F32),
            jax.ShapeDtypeStruct((rank, columns), F32),
        ],
        in_specs=[pl.BlockSpec(memory_space=pltpu.HBM)] * 6,
        out_specs=[
            pl.BlockSpec(memory_space=pl.ANY),
            pl.BlockSpec(memory_space=pl.ANY),
            pl.BlockSpec(memory_space=pltpu.VMEM),
        ],
        scratch_shapes=[
            *(pltpu.VMEM(arg.shape, arg.dtype) for arg in args),
            pltpu.VMEM((levels, *square), F32),
            pltpu.VMEM((levels, *square), F32),
            pltpu.VMEM((2, rank, half), F32),
            pltpu.VMEM((levels, rank, half), F32),
            pltpu.VMEM((levels, rank, half), F32),
            pltpu.VMEM((rank, half), F32),
            pltpu.VMEM((rank, half), F32),
            pltpu.VMEM((levels, *square), BF16),
            pltpu.VMEM((levels, *square), BF16),
            pltpu.VMEM((levels, *square), BF16),
            pltpu.VMEM((levels, *square), BF16),
            pltpu.VMEM((levels, *square), F32),
            pltpu.VMEM((4, *square), BF16),
            pltpu.VMEM((2, *square), BF16),
            pltpu.VMEM((rank, half), F32),
            pltpu.VMEM(square, F32),
            pltpu.VMEM((rank, half), F32),
            pltpu.VMEM((2, points, half), F32),
            pltpu.VMEM((2, points, rank), BF16),
            pltpu.VMEM((points, rank), F32),
            pltpu.VMEM((points, points), BF16),
            dma((6,)),
            dma((3,)),
            dma((levels, 2)),
            dma((levels,)),
            dma((levels,)),
            dma((levels,)),
            dma((3,)),
            dma((3,)),
        ],
        compiler_params=pltpu.CompilerParams(collective_id=0, has_side_effects=True, vmem_limit_bytes=60 * 2**20),
        name="tree_solve",
    )(*args)
    return z - jnp.dot(q, alpha, precision=lax.Precision.HIGHEST, preferred_element_type=F32)


def solution(mesh):
    placed = (
        P("leaf", "rhs"),
        P("leaf", None),
        P("leaf", None),
        P("leaf", None),
        P("leaf", None, None, None),
        P("leaf", None, None, None),
    )
    return jax.shard_map(
        body, mesh=mesh, in_specs=placed, out_specs=P("leaf", "rhs"), check_vma=False
    )
```
